512 devices in a mesh: sta: 128 (over z_hi, x, y), tm: 4 (over z_lo, core).
Axes of the slice: x: 4, y: 8, z: 8 (z_hi: 4, z_lo: 2; z = z_hi * 2 + z_lo), core: 2. Of those that a mesh axis runs over, the one named last changes fastest.
Arguments:
- records: bfloat16 [16384, 1024], P('sta', 'tm'), may hold values from -6 to 6
- filter_taps: float32 [127], replicated, may hold values from -0.5 to 0.5
- plan: int32 [3], replicated, may hold values from 1 to 127, as said below
- station_valid: int32 [16384], P('sta'), may hold values 0 or 1
Outputs:
- correlations: bfloat16 [3, 16384, 101, 128], P(None, ('sta', 'tm'))
The draws below stay inside these ranges and needn't reach their ends.
Inputs may be any that keep to these rules, and one draw needn't show every extreme that they name: `plan`: the 3 distances are distinct, and one of them is 127.
All inputs are finite; a program needn't handle non-finite values. No bound on the sum of `station_valid` on one device may be relied on, other than what follows from the above.
Results may differ from the reference program's by a relative error of at most 0.0048.
Values may be sent and summed in bfloat16 or wider, within the bound.
No kernel may reach another device: no remote copies, remote signals or barrier semaphores. Data moves between devices by JAX's collectives and lax.ppermute only.
A program may use at most 64 MiB of HBM per device.

```python
import jax
import jax.numpy as jnp
from jax import lax

STA_DEV = 128
SAMPLES = 1024
TAPS = 127
AVG_HALF = 64
LAGS = 101
ROUNDS = 3
BLOCKS = 128
STATIONS = 16384


def draw_plan(key, part):
    first_key = jax.random.fold_in(key, 11)
    second_key = jax.random.fold_in(key, 23)
    shuffled = jax.random.permutation(first_key, BLOCKS - 2) + 1
    chosen = jnp.concatenate([jnp.array([BLOCKS - 1], jnp.int32), shuffled[:ROUNDS - 1].astype(jnp.int32)])
    placing = jax.random.permutation(second_key, ROUNDS)
    return chosen[placing].astype(jnp.int32)


def with_ends(values, own_key, smallest, largest):
    longest = values.shape.index(max(values.shape))
    spots = []
    for shift in (0, 1):
        where = [jax.random.randint(jax.random.fold_in(own_key, axis), (), 0, length) for axis, length in enumerate(values.shape)]
        where[longest] = (where[longest] + shift) % values.shape[longest]
        spots.append(tuple(where))
    return values.at[spots[0]].set(smallest).at[spots[1]].set(largest)


def block_levels(key, shape, split, least, high):
    gain = 1.0
    for position, blocks in split:
        heights = jax.random.uniform(jax.random.fold_in(jax.random.fold_in(key, 6), position), (blocks,), jnp.float32, least / len(split), high / len(split))
        gain = gain * jnp.repeat(jnp.exp(heights), shape[position] // blocks).reshape((-1,) + (1,) * (len(shape) - 1 - position))
    return gain


def normal_values(rng, extent, scale, most, cuts=(), held_as=jnp.bfloat16):
    drawn = scale * jax.random.normal(rng, extent, jnp.float32)
    if cuts:
        drawn = drawn * block_levels(rng, extent, cuts, -0.22, 0.18)
    return jnp.clip(drawn, -most, most).astype(held_as)


def setup_inputs(seed: int = 0) -> dict:
    key_list = jax.random.split(jax.random.key(seed), 5)
    return {
        "records": normal_values(key_list[0], (STATIONS, SAMPLES), 1.0, 6.0, ((0, 128), (1, 4))),
        "filter_taps": normal_values(key_list[1], (TAPS,), TAPS ** -0.5, 0.5, (), jnp.float32),
        "plan": draw_plan(jax.random.fold_in(key_list[4], 71), 0),
        "station_valid": with_ends((jax.random.randint(key_list[3], (STATIONS,), 0, 8) < 7).astype(jnp.int32), jax.random.fold_in(key_list[3], 1), 0, 1),
    }


def reference(records, filter_taps, plan, station_valid):
    half_taps = (TAPS - 1) // 2
    half_lags = (LAGS - 1) // 2
    signal = records.astype(jnp.float32)
    padded = jnp.pad(signal, ((0, 0), (half_taps, half_taps)))
    filtered = jnp.zeros_like(signal)
    for k in range(TAPS):
        filtered = filtered + filter_taps[k] * padded[:, k:k + SAMPLES]
    magnitude_pad = jnp.pad(jnp.abs(filtered), ((0, 0), (AVG_HALF, AVG_HALF)))
    magnitude_sum = lax.reduce_window(magnitude_pad, jnp.zeros((), filtered.dtype), lax.add, (1, 2 * AVG_HALF + 1), (1, 1), 'VALID')
    magnitude = magnitude_sum / (2 * AVG_HALF + 1) + 1e-05
    normalized = (filtered / magnitude * station_valid[:, None].astype(jnp.float32)).astype(jnp.bfloat16)
    blocks = normalized.astype(jnp.float32).reshape(BLOCKS, STA_DEV, SAMPLES)
    padded_blocks = jnp.pad(blocks, ((0, 0), (0, 0), (half_lags, half_lags)))
    factor = 1.0 / jnp.sqrt(jnp.float32(SAMPLES))

    def one_round(distance):

        def one_block(index):
            own_rows = blocks[index]
            partner = padded_blocks[jnp.bitwise_xor(index, distance)]
            windows = jnp.stack([partner[:, l:l + SAMPLES] for l in range(LAGS)])
            return jnp.einsum('it,ljt->ilj', own_rows, windows, precision=lax.Precision.HIGHEST)
        values = lax.map(one_block, jnp.arange(BLOCKS, dtype=jnp.int32))
        return (values.reshape(STATIONS, LAGS, STA_DEV) * factor).astype(jnp.bfloat16)
    results = [one_round(plan[r].astype(jnp.int32)) for r in range(ROUNDS)]
    return jnp.stack(results)
```

```python
import functools

import jax
import jax.numpy as jnp
from jax import lax
from jax.experimental import pallas as pl
from jax.experimental.pallas import tpu as pltpu
from jax.sharding import PartitionSpec as P

TAPS = 127
AVG_HALF = 64
LAGS = 101
HALF_LAGS = 50
SAMPLES = 1024
STA_DEV = 128
OWN = 32
ROUNDS = 3
SIDE = 128
TILE = 256
SPAN = TILE + 2 * SIDE
WIDE = SAMPLES + SIDE
LAG_STEP = 26
LEAD_GAP = SIDE // 2 - HALF_LAGS
ROLL_DTYPE = jnp.bfloat16
NT = (((1,), (1,)), ((), ()))


def dot_nt(a, b):
    return lax.dot_general(a, b, NT, preferred_element_type=jnp.float32)


def split_bf16(value):
    high = value.astype(jnp.bfloat16)
    low = (value - high.astype(jnp.float32)).astype(jnp.bfloat16)
    return high, low


def bands(taps_row):
    spread = jnp.broadcast_to(taps_row, (TILE, SPAN))
    rolled = pltpu.roll(spread, SIDE - (TAPS - 1) // 2, 1, stride=1, stride_axis=0)
    high, low = split_bf16(rolled)
    out_pos = lax.broadcasted_iota(jnp.int32, (TILE, SPAN), 0)
    in_pos = lax.broadcasted_iota(jnp.int32, (TILE, SPAN), 1)
    offset = in_pos - out_pos - SIDE
    inside = (offset >= -AVG_HALF) & (offset <= AVG_HALF)
    return high, low, jnp.where(inside, 1.0, 0.0).astype(jnp.bfloat16)


def normalize_rows(raw, high, low, ones):
    rows = raw.shape[0]
    side = jnp.zeros((rows, SIDE), jnp.bfloat16)
    extended = jnp.concatenate([side, raw, side], axis=1)
    parts = []
    for c in range(SAMPLES // TILE):
        window = extended[:, TILE * c : TILE * c + SPAN]
        parts.append(dot_nt(window, high) + dot_nt(window, low))
    filtered = jnp.concatenate(parts, axis=1)
    abs_high, abs_low = split_bf16(jnp.abs(filtered))
    abs_high = jnp.concatenate([side, abs_high, side], axis=1)
    abs_low = jnp.concatenate([side, abs_low, side], axis=1)
    parts = []
    for c in range(SAMPLES // TILE):
        s = slice(TILE * c, TILE * c + SPAN)
        parts.append(dot_nt(abs_high[:, s], ones) + dot_nt(abs_low[:, s], ones))
    magnitude = jnp.concatenate(parts, axis=1) / (2 * AVG_HALF + 1) + 1e-05
    return (filtered / magnitude).astype(jnp.bfloat16)


def shift_windows(own_ext, lag):
    start = SIDE - LEAD_GAP - lag
    lanes = lax.broadcasted_iota(jnp.int32, (OWN, SIDE), 1)
    near = lanes < SIDE - start
    rolled = [
        pltpu.roll(own_ext[:, SIDE * c : SIDE * (c + 1)], SIDE - start, 1)
        for c in range(WIDE // SIDE)
    ]
    return [jnp.where(near, rolled[c], rolled[c + 1]) for c in range(SAMPLES // SIDE)]


def correlate_kernel(order_ref, taps_ref, own_ref, part_ref, out_ref, own_norm, part_norm, shifted):
    step = pl.program_id(0)

    @pl.when(step == 0)
    def _():
        high, low, ones = bands(taps_ref[...])
        own = jnp.concatenate([own_ref[t] for t in range(4)], axis=1)
        own = normalize_rows(own, high, low, ones).astype(jnp.float32)
        lead = jnp.zeros((OWN, SIDE // 2), jnp.float32)
        own_norm[...] = jnp.concatenate([lead, own, lead], axis=1).astype(ROLL_DTYPE)
        for r in range(ROUNDS):
            raw = jnp.concatenate([part_ref[t, r] for t in range(4)], axis=1)
            part_norm[r * STA_DEV : (r + 1) * STA_DEV, :] = normalize_rows(raw, high, low, ones)

    for k in range(LAG_STEP):
        windows = shift_windows(own_norm, step * LAG_STEP + k)
        for c, window in enumerate(windows):
            shifted[k * OWN : (k + 1) * OWN, SIDE * c : SIDE * (c + 1)] = window.astype(jnp.bfloat16)
    sums = dot_nt(shifted[...], part_norm[...]) * (1.0 / 32.0)
    for slot in range(ROUNDS):
        block = sums[:, slot * STA_DEV : (slot + 1) * STA_DEV].astype(jnp.bfloat16)
        out_ref[order_ref[slot]] = block.reshape(LAG_STEP, OWN, STA_DEV)


def correlate(order, taps_row, own, parts):
    by_lag = pl.pallas_call(
        correlate_kernel,
        out_shape=jax.ShapeDtypeStruct((ROUNDS, LAGS, OWN, STA_DEV), jnp.bfloat16),
        grid_spec=pltpu.PrefetchScalarGridSpec(
            num_scalar_prefetch=1,
            grid=(pl.cdiv(LAGS, LAG_STEP),),
            in_specs=[
                pl.BlockSpec((1, SPAN), lambda i, order: (0, 0)),
                pl.BlockSpec((4, OWN, TILE), lambda i, order: (0, 0, 0)),
                pl.BlockSpec((4, ROUNDS, STA_DEV, TILE), lambda i, order: (0, 0, 0, 0)),
            ],
            out_specs=pl.BlockSpec(
                (ROUNDS, LAG_STEP, OWN, STA_DEV), lambda i, order: (0, i, 0, 0)
            ),
            scratch_shapes=[
                pltpu.VMEM((OWN, WIDE), ROLL_DTYPE),
                pltpu.VMEM((ROUNDS * STA_DEV, SAMPLES), jnp.bfloat16),
                pltpu.VMEM((LAG_STEP * OWN, SAMPLES), jnp.bfloat16),
            ],
        ),
        name="correlate",
    )(order, taps_row, own, parts)
    return jnp.transpose(by_lag, (0, 2, 1, 3))


def exchange(value, distance):
    if distance == 0:
        return value
    pairs = [(s, s ^ distance) for s in range(lax.axis_size("sta"))]
    return lax.ppermute(value, "sta", pairs)


def route(value, distance, low_bits, bits):
    count = 2**bits
    branches = [functools.partial(exchange, distance=k << low_bits) for k in range(count)]
    return lax.switch((distance >> low_bits) & (count - 1), branches, value)


def local(records, filter_taps, plan, station_valid):
    farthest = lax.axis_size("sta") - 1
    masked = records * station_valid[:, None].astype(jnp.bfloat16)
    far = exchange(masked, farthest)
    first = jnp.where(plan[0] == farthest, plan[1], plan[0])
    second = jnp.where(plan[2] == farthest, plan[1], plan[2])
    routed = [far]
    for distance in (first, second):
        routed.append(route(route(masked, distance, 0, 3), distance, 3, 4))
    far_round = jnp.where(plan[0] == farthest, 0, jnp.where(plan[1] == farthest, 1, 2))
    order = jnp.stack(
        [far_round, jnp.where(far_round == 0, 1, 0), jnp.where(far_round == 2, 1, 2)]
    ).astype(jnp.int32)
    own = lax.all_to_all(
        masked.reshape(4, OWN, TILE), "tm", split_axis=0, concat_axis=0, tiled=True
    )
    parts = lax.all_gather(jnp.stack(routed), "tm")
    taps_row = jnp.pad(filter_taps, (0, SPAN - TAPS)).reshape(1, SPAN)
    return correlate(order, taps_row, own, parts)


def solution(mesh):
    return jax.shard_map(
        local,
        mesh=mesh,
        in_specs=(P("sta", "tm"), P(), P(), P("sta")),
        out_specs=P(None, ("sta", "tm"), None, None),
        check_vma=False,
    )
```

```python
import functools

import jax
import jax.numpy as jnp
from jax import lax
from jax.experimental import pallas as pl
from jax.experimental.pallas import tpu as pltpu
from jax.sharding import PartitionSpec as P

TAPS = 127
AVG_HALF = 64
LAGS = 101
HALF_LAGS = 50
SAMPLES = 1024
STA_DEV = 128
OWN = 32
ROUNDS = 3
SIDE = 128
TILE = 256
SPAN = TILE + 2 * SIDE
WIDE = SAMPLES + SIDE
LAG_STEP = 26
LEAD_GAP = SIDE // 2 - HALF_LAGS
TM = 4
BLOCKS = 128
FARTHEST = BLOCKS - 1
NT = (((1,), (1,)), ((), ()))


def dot_nt(a, b):
    return lax.dot_general(a, b, NT, preferred_element_type=jnp.float32)


def split_bf16(value):
    high = value.astype(jnp.bfloat16)
    low = (value - high.astype(jnp.float32)).astype(jnp.bfloat16)
    return high, low


def bands(taps_row):
    padded = jnp.concatenate([taps_row, jnp.zeros((1, SPAN - TAPS), jnp.float32)], axis=1)
    spread = jnp.broadcast_to(padded, (TILE, SPAN))
    rolled = pltpu.roll(spread, SIDE - (TAPS - 1) // 2, 1, stride=1, stride_axis=0)
    high, low = split_bf16(rolled)
    out_pos = lax.broadcasted_iota(jnp.int32, (TILE, SPAN), 0)
    in_pos = lax.broadcasted_iota(jnp.int32, (TILE, SPAN), 1)
    offset = in_pos - out_pos - SIDE
    inside = (offset >= -AVG_HALF) & (offset <= AVG_HALF)
    return high, low, jnp.where(inside, 1.0, 0.0).astype(jnp.bfloat16)


def stacked_windows(series):
    side = jnp.zeros((series.shape[0], SIDE), series.dtype)
    extended = jnp.concatenate([side, series, side], axis=1)
    tiles = [extended[:, TILE * c : TILE * c + SPAN] for c in range(SAMPLES // TILE)]
    return jnp.concatenate(tiles, axis=0)


def unstacked(tiles, rows):
    return jnp.concatenate(
        [tiles[rows * c : rows * (c + 1)] for c in range(SAMPLES // TILE)], axis=1
    )


def normalize_rows(raw, high, low, ones):
    rows = raw.shape[0]
    windows = stacked_windows(raw)
    filtered = unstacked(dot_nt(windows, high) + dot_nt(windows, low), rows)
    abs_high, abs_low = split_bf16(jnp.abs(filtered))
    total = dot_nt(stacked_windows(abs_high), ones) + dot_nt(stacked_windows(abs_low), ones)
    magnitude = unstacked(total, rows) / (2 * AVG_HALF + 1) + 1e-05
    return (filtered / magnitude).astype(jnp.bfloat16)


def shift_windows(own_ext, lag):
    start = SIDE - LEAD_GAP - lag
    lanes = lax.broadcasted_iota(jnp.int32, (OWN, SIDE), 1)
    near = lanes < SIDE - start
    rolled = [
        pltpu.roll(own_ext[:, SIDE * c : SIDE * (c + 1)], SIDE - start, 1)
        for c in range(WIDE // SIDE)
    ]
    return [jnp.where(near, rolled[c], rolled[c + 1]) for c in range(SAMPLES // SIDE)]


def correlate_kernel(
    order_ref, taps_ref, own_ref, blocks_ref, out_ref, own_norm, part_norm, shifted
):
    step = pl.program_id(0)

    @pl.when(step == 0)
    def _():
        high, low, ones = bands(taps_ref[...])
        series = [
            jnp.concatenate([blocks_ref[t, r] for t in range(TM)], axis=1) for r in range(ROUNDS)
        ]
        series.append(jnp.concatenate([own_ref[t] for t in range(TM)], axis=1))
        normalized = normalize_rows(jnp.concatenate(series, axis=0), high, low, ones)
        part_norm[...] = normalized[: ROUNDS * STA_DEV]
        own = normalized[ROUNDS * STA_DEV :].astype(jnp.float32)
        lead = jnp.zeros((OWN, SIDE // 2), jnp.float32)
        own_norm[...] = jnp.concatenate([lead, own, lead], axis=1).astype(jnp.bfloat16)

    for k in range(LAG_STEP):
        windows = shift_windows(own_norm, step * LAG_STEP + k)
        for c, window in enumerate(windows):
            shifted[k * OWN : (k + 1) * OWN, SIDE * c : SIDE * (c + 1)] = window.astype(jnp.bfloat16)
    sums = dot_nt(shifted[...], part_norm[...]) * (1.0 / 32.0)
    for slot in range(ROUNDS):
        block = sums[:, slot * STA_DEV : (slot + 1) * STA_DEV].astype(jnp.bfloat16)
        out_ref[order_ref[slot]] = block.reshape(LAG_STEP, OWN, STA_DEV)


def correlate(order, taps_row, own, blocks):
    by_lag = pl.pallas_call(
        correlate_kernel,
        out_shape=jax.ShapeDtypeStruct((ROUNDS, LAGS, OWN, STA_DEV), jnp.bfloat16),
        grid_spec=pltpu.PrefetchScalarGridSpec(
            num_scalar_prefetch=1,
            grid=(pl.cdiv(LAGS, LAG_STEP),),
            in_specs=[
                pl.BlockSpec((1, TAPS), lambda i, order: (0, 0)),
                pl.BlockSpec((TM, OWN, TILE), lambda i, order: (0, 0, 0)),
                pl.BlockSpec((TM, ROUNDS, STA_DEV, TILE), lambda i, order: (0, 0, 0, 0)),
            ],
            out_specs=pl.BlockSpec(
                (ROUNDS, LAG_STEP, OWN, STA_DEV), lambda i, order: (0, i, 0, 0)
            ),
            scratch_shapes=[
                pltpu.VMEM((OWN, WIDE), jnp.bfloat16),
                pltpu.VMEM((ROUNDS * STA_DEV, SAMPLES), jnp.bfloat16),
                pltpu.VMEM((LAG_STEP * OWN, SAMPLES), jnp.bfloat16),
            ],
        ),
        name="correlate",
    )(order, taps_row, own, blocks)
    return jnp.transpose(by_lag, (0, 2, 1, 3))


def prepare_kernel(plan_ref, valid_ref, records_ref, masked_ref, pair_ref, low_ref, top_ref, order_ref):
    far = jnp.where(plan_ref[0] == FARTHEST, 0, jnp.where(plan_ref[1] == FARTHEST, 1, 2))
    first = jnp.where(far == 0, 1, 0)
    second = jnp.where(far == 2, 1, 2)
    first_bits = jnp.where(far == 0, plan_ref[1], plan_ref[0])
    second_bits = jnp.where(far == 2, plan_ref[1], plan_ref[2])
    swap = (first_bits & 7) > (second_bits & 7)
    low = jnp.where(swap, second_bits, first_bits)
    top = jnp.where(swap, first_bits, second_bits)
    a = low & 7
    pair_ref[0] = a * 8 - ((a * (a - 1)) >> 1) + (top & 7) - a
    low_ref[0] = low >> 3
    top_ref[0] = top >> 3
    order_ref[0] = far
    order_ref[1] = jnp.where(swap, second, first)
    order_ref[2] = jnp.where(swap, first, second)
    row = lax.broadcasted_iota(jnp.int32, (STA_DEV, STA_DEV), 0)
    col = lax.broadcasted_iota(jnp.int32, (STA_DEV, STA_DEV), 1)
    flags = jnp.where(row == col, valid_ref[...].astype(jnp.float32), 0.0).astype(jnp.bfloat16)
    masked_ref[...] = jnp.dot(
        flags, records_ref[...], preferred_element_type=jnp.float32
    ).astype(jnp.bfloat16)


def prepare(plan, valid, records):
    smem = pl.BlockSpec(memory_space=pltpu.SMEM)
    vmem = pl.BlockSpec(memory_space=pltpu.VMEM)
    scalar = jax.ShapeDtypeStruct((1,), jnp.int32)
    return pl.pallas_call(
        prepare_kernel,
        out_shape=(
            jax.ShapeDtypeStruct(records.shape, jnp.bfloat16),
            scalar,
            scalar,
            scalar,
            jax.ShapeDtypeStruct((ROUNDS,), jnp.int32),
        ),
        in_specs=[smem, vmem, vmem],
        out_specs=(vmem, smem, smem, smem, smem),
        name="prepare",
    )(plan, valid.reshape(1, STA_DEV), records)


def exchange(value, distance):
    if distance == 0:
        return value
    pairs = [(s, s ^ distance) for s in range(BLOCKS)]
    return lax.ppermute(value, "sta", pairs)


def low_bits_pair(value, index):
    def branch(value, near, other):
        low = exchange(value, near)
        return low, low if near == other else exchange(value, other)

    branches = [
        functools.partial(branch, near=i, other=j) for i in range(8) for j in range(i, 8)
    ]
    return lax.switch(index, branches, value)


def high_bits(value, index):
    return lax.switch(
        index, [functools.partial(exchange, distance=k << 3) for k in range(BLOCKS >> 3)], value
    )


def local(records, filter_taps, plan, station_valid):
    masked, pair, low_index, top_index, order = prepare(plan, station_valid, records)
    far = exchange(masked, FARTHEST)
    low, top = low_bits_pair(masked, pair.reshape(()))
    low = high_bits(low, low_index.reshape(()))
    top = high_bits(top, top_index.reshape(()))
    own = lax.all_to_all(
        masked.reshape(TM, OWN, TILE), "tm", split_axis=0, concat_axis=0, tiled=True
    )
    blocks = lax.all_gather(jnp.stack([far, low, top]), "tm")
    return correlate(order, filter_taps.reshape(1, TAPS), own, blocks)


def solution(mesh):
    return jax.shard_map(
        local,
        mesh=mesh,
        in_specs=(P("sta", "tm"), P(), P(), P("sta")),
        out_specs=P(None, ("sta", "tm"), None, None),
        check_vma=False,
    )
```

```python
import functools

import jax
import jax.numpy as jnp
from jax import lax
from jax.experimental import pallas as pl
from jax.experimental.pallas import tpu as pltpu
from jax.sharding import PartitionSpec as P

TAPS = 127
AVG_HALF = 64
LAGS = 101
HALF_LAGS = 50
SAMPLES = 1024
STA_DEV = 128
OWN = 32
ROUNDS = 3
SIDE = 128
TILE = 256
SPAN = TILE + 2 * SIDE
WIDE = SAMPLES + SIDE
LAG_STEP = 26
LEAD_GAP = SIDE // 2 - HALF_LAGS
TM = 4
BLOCKS = 128
FARTHEST = BLOCKS - 1
NT = (((1,), (1,)), ((), ()))


def dot_nt(a, b):
    return lax.dot_general(a, b, NT, preferred_element_type=jnp.float32)


def split_bf16(value):
    high = value.astype(jnp.bfloat16)
    low = (value - high.astype(jnp.float32)).astype(jnp.bfloat16)
    return high, low


def bands(taps_row):
    padded = jnp.concatenate([taps_row, jnp.zeros((1, SPAN - TAPS), jnp.float32)], axis=1)
    spread = jnp.broadcast_to(padded, (TILE, SPAN))
    rolled = pltpu.roll(spread, SIDE - (TAPS - 1) // 2, 1, stride=1, stride_axis=0)
    high, low = split_bf16(rolled)
    out_pos = lax.broadcasted_iota(jnp.int32, (TILE, SPAN), 0)
    in_pos = lax.broadcasted_iota(jnp.int32, (TILE, SPAN), 1)
    offset = in_pos - out_pos - SIDE
    inside = (offset >= -AVG_HALF) & (offset <= AVG_HALF)
    taps = jnp.concatenate([high, low], axis=1)
    return taps, jnp.where(inside, 1.0, 0.0).astype(jnp.bfloat16)


def stacked_windows(series):
    side = jnp.zeros((series.shape[0], SIDE), series.dtype)
    extended = jnp.concatenate([side, series, side], axis=1)
    tiles = [extended[:, TILE * c : TILE * c + SPAN] for c in range(SAMPLES // TILE)]
    return jnp.concatenate(tiles, axis=0)


def unstacked(tiles, rows):
    return jnp.concatenate(
        [tiles[rows * c : rows * (c + 1)] for c in range(SAMPLES // TILE)], axis=1
    )


def normalize_rows(raw, taps, ones):
    rows = raw.shape[0]
    windows = stacked_windows(raw)
    filtered = unstacked(dot_nt(jnp.concatenate([windows, windows], axis=1), taps), rows)
    halves = [stacked_windows(half) for half in split_bf16(jnp.abs(filtered))]
    total = dot_nt(jnp.concatenate(halves, axis=1), jnp.concatenate([ones, ones], axis=1))
    magnitude = unstacked(total, rows) / (2 * AVG_HALF + 1) + 1e-05
    return (filtered / magnitude).astype(jnp.bfloat16)


def shift_windows(own_ext, lag):
    start = SIDE - LEAD_GAP - lag
    lanes = lax.broadcasted_iota(jnp.int32, (OWN, SIDE), 1)
    near = lanes < SIDE - start
    rolled = [
        pltpu.roll(own_ext[:, SIDE * c : SIDE * (c + 1)], SIDE - start, 1)
        for c in range(WIDE // SIDE)
    ]
    return [jnp.where(near, rolled[c], rolled[c + 1]) for c in range(SAMPLES // SIDE)]


def correlate_kernel(
    order_ref, taps_ref, own_ref, blocks_ref, out_ref, own_norm, part_norm, shifted
):
    step = pl.program_id(0)

    @pl.when(step == 0)
    def _():
        taps, ones = bands(taps_ref[...])
        series = [
            jnp.concatenate([blocks_ref[t, r] for t in range(TM)], axis=1) for r in range(ROUNDS)
        ]
        series.append(jnp.concatenate([own_ref[t] for t in range(TM)], axis=1))
        normalized = normalize_rows(jnp.concatenate(series, axis=0), taps, ones)
        part_norm[...] = normalized[: ROUNDS * STA_DEV]
        own = normalized[ROUNDS * STA_DEV :].astype(jnp.float32)
        lead = jnp.zeros((OWN, SIDE // 2), jnp.float32)
        own_norm[...] = jnp.concatenate([lead, own, lead], axis=1).astype(jnp.bfloat16)

    for k in range(LAG_STEP):
        windows = shift_windows(own_norm, step * LAG_STEP + k)
        for c, window in enumerate(windows):
            shifted[k * OWN : (k + 1) * OWN, SIDE * c : SIDE * (c + 1)] = window.astype(jnp.bfloat16)
    sums = dot_nt(shifted[...], part_norm[...]) * (1.0 / 32.0)
    for slot in range(ROUNDS):
        block = sums[:, slot * STA_DEV : (slot + 1) * STA_DEV].astype(jnp.bfloat16)
        out_ref[order_ref[slot]] = block.reshape(LAG_STEP, OWN, STA_DEV)


def correlate(order, taps_row, own, blocks):
    by_lag = pl.pallas_call(
        correlate_kernel,
        out_shape=jax.ShapeDtypeStruct((ROUNDS, LAGS, OWN, STA_DEV), jnp.bfloat16),
        grid_spec=pltpu.PrefetchScalarGridSpec(
            num_scalar_prefetch=1,
            grid=(pl.cdiv(LAGS, LAG_STEP),),
            in_specs=[
                pl.BlockSpec((1, TAPS), lambda i, order: (0, 0)),
                pl.BlockSpec((TM, OWN, TILE), lambda i, order: (0, 0, 0)),
                pl.BlockSpec((TM, ROUNDS, STA_DEV, TILE), lambda i, order: (0, 0, 0, 0)),
            ],
            out_specs=pl.BlockSpec(
                (ROUNDS, LAG_STEP, OWN, STA_DEV), lambda i, order: (0, i, 0, 0)
            ),
            scratch_shapes=[
                pltpu.VMEM((OWN, WIDE), jnp.bfloat16),
                pltpu.VMEM((ROUNDS * STA_DEV, SAMPLES), jnp.bfloat16),
                pltpu.VMEM((LAG_STEP * OWN, SAMPLES), jnp.bfloat16),
            ],
        ),
        compiler_params=pltpu.CompilerParams(vmem_limit_bytes=24 << 20),
        name="correlate",
    )(order, taps_row, own, blocks)
    return jnp.transpose(by_lag, (0, 2, 1, 3))


def prepare_kernel(plan_ref, valid_ref, records_ref, masked_ref, pair_ref, low_ref, top_ref, order_ref):
    far = jnp.where(plan_ref[0] == FARTHEST, 0, jnp.where(plan_ref[1] == FARTHEST, 1, 2))
    first = jnp.where(far == 0, 1, 0)
    second = jnp.where(far == 2, 1, 2)
    first_bits = jnp.where(far == 0, plan_ref[1], plan_ref[0])
    second_bits = jnp.where(far == 2, plan_ref[1], plan_ref[2])
    swap = (first_bits & 7) > (second_bits & 7)
    low = jnp.where(swap, second_bits, first_bits)
    top = jnp.where(swap, first_bits, second_bits)
    a = low & 7
    pair_ref[0] = a * 8 - ((a * (a - 1)) >> 1) + (top & 7) - a
    low_ref[0] = low >> 3
    top_ref[0] = top >> 3
    order_ref[0] = far
    order_ref[1] = jnp.where(swap, second, first)
    order_ref[2] = jnp.where(swap, first, second)
    row = lax.broadcasted_iota(jnp.int32, (STA_DEV, STA_DEV), 0)
    col = lax.broadcasted_iota(jnp.int32, (STA_DEV, STA_DEV), 1)
    flags = jnp.where(row == col, valid_ref[...].astype(jnp.float32), 0.0).astype(jnp.bfloat16)
    masked_ref[...] = jnp.dot(
        flags, records_ref[...], preferred_element_type=jnp.float32
    ).astype(jnp.bfloat16)


def prepare(plan, valid, records):
    smem = pl.BlockSpec(memory_space=pltpu.SMEM)
    vmem = pl.BlockSpec(memory_space=pltpu.VMEM)
    scalar = jax.ShapeDtypeStruct((1,), jnp.int32)
    return pl.pallas_call(
        prepare_kernel,
        out_shape=(
            jax.ShapeDtypeStruct(records.shape, jnp.bfloat16),
            scalar,
            scalar,
            scalar,
            jax.ShapeDtypeStruct((ROUNDS,), jnp.int32),
        ),
        in_specs=[smem, vmem, vmem],
        out_specs=(vmem, smem, smem, smem, smem),
        name="prepare",
    )(plan, valid.reshape(1, STA_DEV), records)


def exchange(value, distance):
    if distance == 0:
        return value
    pairs = [(s, s ^ distance) for s in range(BLOCKS)]
    return lax.ppermute(value, "sta", pairs)


def select_branch(index, branches, *operands):
    traced = jax.make_jaxpr(lambda *args: lax.switch(args[0], branches, *args[1:]))(index, *operands)
    (cond,) = [eqn for eqn in traced.eqns if eqn.primitive.name == "cond"]
    return cond.primitive.bind(index, *operands, **cond.params)


def low_bits_pair(value, index):
    def branch(value, near, other):
        low = exchange(value, near)
        return low, low if near == other else exchange(value, other)

    branches = [
        functools.partial(branch, near=i, other=j) for i in range(8) for j in range(i, 8)
    ]
    return select_branch(index, branches, value)


def high_bits(value, index):
    branches = [functools.partial(exchange, distance=k << 3) for k in range(BLOCKS >> 3)]
    return select_branch(index, branches, value)[0]


def own_series(masked):
    return lax.all_to_all(
        masked.reshape(TM, OWN, TILE), "tm", split_axis=0, concat_axis=0, tiled=True
    )


def high_bits_and_own(value, index, masked):
    def branch(value, masked, distance):
        moved = exchange(value, distance)
        return moved, own_series(masked)

    branches = [functools.partial(branch, distance=k << 3) for k in range(BLOCKS >> 3)]
    return select_branch(index, branches, value, masked)


def local(records, filter_taps, plan, station_valid):
    masked, pair, low_index, top_index, order = prepare(plan, station_valid, records)
    far = exchange(masked, FARTHEST)
    low, top = low_bits_pair(masked, pair.reshape(()))
    low, own = high_bits_and_own(low, low_index.reshape(()), masked)
    top = high_bits(top, top_index.reshape(()))
    blocks = lax.all_gather(jnp.stack([far, low, top]), "tm")
    return correlate(order, filter_taps.reshape(1, TAPS), own, blocks)


def solution(mesh):
    return jax.shard_map(
        local,
        mesh=mesh,
        in_specs=(P("sta", "tm"), P(), P(), P("sta")),
        out_specs=P(None, ("sta", "tm"), None, None),
        check_vma=False,
    )
```

```python
import functools

import jax
import jax.numpy as jnp
from jax import lax
from jax.experimental import pallas as pl
from jax.experimental.pallas import tpu as pltpu
from jax.sharding import PartitionSpec as P

TAPS = 127
AVG_HALF = 64
LAGS = 101
HALF_LAGS = 50
SAMPLES = 1024
STA_DEV = 128
OWN = 32
ROUNDS = 3
SIDE = 128
TILE = 256
EDGE = SIDE // 2
SPAN = TILE + 2 * EDGE
WIDE = SAMPLES + SIDE
LAG_STEP = 51
LEAD_GAP = SIDE // 2 - HALF_LAGS
TM = 4
BLOCKS = 128
FARTHEST = BLOCKS - 1
SENT = ROUNDS * STA_DEV + STA_DEV - OWN
NT = (((1,), (1,)), ((), ()))


def dot_nt(a, b):
    return lax.dot_general(a, b, NT, preferred_element_type=jnp.float32)


def split_bf16(value):
    high = value.astype(jnp.bfloat16)
    low = (value - high.astype(jnp.float32)).astype(jnp.bfloat16)
    return high, low


def bands(taps_row):
    width = 2 * TILE
    padded = jnp.concatenate([taps_row, jnp.zeros((1, width - TAPS), jnp.float32)], axis=1)
    spread = jnp.broadcast_to(padded, (TILE, width))
    rolled = pltpu.roll(spread, EDGE - (TAPS - 1) // 2, 1, stride=1, stride_axis=0)
    taps = jnp.concatenate(split_bf16(rolled[:, :SPAN]), axis=1)
    out_pos = lax.broadcasted_iota(jnp.int32, (TILE, SPAN), 0)
    in_pos = lax.broadcasted_iota(jnp.int32, (TILE, SPAN), 1)
    offset = in_pos - out_pos - EDGE
    inside = (offset >= -AVG_HALF) & (offset <= AVG_HALF)
    ones = jnp.where(inside, 1.0, 0.0).astype(jnp.bfloat16)
    return taps, jnp.concatenate([ones, ones], axis=1)


def stacked_windows(series):
    edge = jnp.zeros((series.shape[0], EDGE), series.dtype)
    extended = jnp.concatenate([edge, series, edge], axis=1)
    tiles = [extended[:, TILE * c : TILE * c + SPAN] for c in range(SAMPLES // TILE)]
    return jnp.concatenate(tiles, axis=0)


def unstacked(tiles, rows):
    return jnp.concatenate(
        [tiles[rows * c : rows * (c + 1)] for c in range(SAMPLES // TILE)], axis=1
    )


def normalize_rows(raw, taps, ones):
    rows = raw.shape[0]
    windows = stacked_windows(raw)
    filtered = unstacked(dot_nt(jnp.concatenate([windows, windows], axis=1), taps), rows)
    halves = [stacked_windows(half) for half in split_bf16(jnp.abs(filtered))]
    total = dot_nt(jnp.concatenate(halves, axis=1), ones)
    magnitude = unstacked(total, rows) / (2 * AVG_HALF + 1) + 1e-05
    return (filtered / magnitude).astype(jnp.bfloat16)


def shift_windows(own_ext, lag):
    start = SIDE - LEAD_GAP - lag
    lanes = lax.broadcasted_iota(jnp.int32, (OWN, SIDE), 1)
    near = lanes < SIDE - start
    rolled = [
        pltpu.roll(own_ext[:, SIDE * c : SIDE * (c + 1)], SIDE - start, 1)
        for c in range(WIDE // SIDE)
    ]
    return [jnp.where(near, rolled[c], rolled[c + 1]) for c in range(SAMPLES // SIDE)]


def correlate_kernel(
    order_ref, taps_ref, mine_ref, blocks_ref, out_ref, own_norm, part_norm, shifted
):
    step = pl.program_id(0)

    @pl.when(step == 0)
    def _():
        taps, ones = bands(taps_ref[...])
        series = [
            jnp.concatenate(
                [blocks_ref[t, r * STA_DEV : (r + 1) * STA_DEV, :] for t in range(TM)], axis=1
            )
            for r in range(ROUNDS)
        ]
        own = []
        for t in range(TM):
            ahead = lax.rem(lax.axis_index("tm") + TM - t, TM)
            place = ROUNDS * STA_DEV + jnp.maximum(ahead - 1, 0) * OWN
            sent = blocks_ref[t, pl.ds(pl.multiple_of(place, OWN), OWN), :]
            own.append(jnp.where(ahead == 0, mine_ref[...], sent))
        series.append(jnp.concatenate(own, axis=1))
        for r in range(ROUNDS):
            part_norm[r * STA_DEV : (r + 1) * STA_DEV, :] = normalize_rows(series[r], taps, ones)
        own = normalize_rows(series[ROUNDS], taps, ones).astype(jnp.float32)
        lead = jnp.zeros((OWN, EDGE), jnp.float32)
        own_norm[...] = jnp.concatenate([lead, own, lead], axis=1).astype(jnp.bfloat16)

    for k in range(LAG_STEP):
        windows = shift_windows(own_norm, step * LAG_STEP + k)
        for c, window in enumerate(windows):
            shifted[k * OWN : (k + 1) * OWN, SIDE * c : SIDE * (c + 1)] = window.astype(jnp.bfloat16)
    sums = dot_nt(shifted[...], part_norm[...]) * (1.0 / 32.0)
    for slot in range(ROUNDS):
        block = sums[:, slot * STA_DEV : (slot + 1) * STA_DEV].astype(jnp.bfloat16)
        out_ref[order_ref[slot]] = block.reshape(LAG_STEP, OWN, STA_DEV)


def correlate(order, taps_row, mine, blocks):
    by_lag = pl.pallas_call(
        correlate_kernel,
        out_shape=jax.ShapeDtypeStruct((ROUNDS, LAGS, OWN, STA_DEV), jnp.bfloat16),
        grid_spec=pltpu.PrefetchScalarGridSpec(
            num_scalar_prefetch=1,
            grid=(pl.cdiv(LAGS, LAG_STEP),),
            in_specs=[
                pl.BlockSpec((1, TAPS), lambda i, order: (0, 0)),
                pl.BlockSpec((OWN, TILE), lambda i, order: (0, 0)),
                pl.BlockSpec((TM, SENT, TILE), lambda i, order: (0, 0, 0)),
            ],
            out_specs=pl.BlockSpec(
                (ROUNDS, LAG_STEP, OWN, STA_DEV), lambda i, order: (0, i, 0, 0)
            ),
            scratch_shapes=[
                pltpu.VMEM((OWN, WIDE), jnp.bfloat16),
                pltpu.VMEM((ROUNDS * STA_DEV, SAMPLES), jnp.bfloat16),
                pltpu.VMEM((LAG_STEP * OWN, SAMPLES), jnp.bfloat16),
            ],
        ),
        compiler_params=pltpu.CompilerParams(vmem_limit_bytes=24 << 20),
        name="correlate",
    )(order, taps_row, mine, blocks)
    return jnp.transpose(by_lag, (0, 2, 1, 3))


def rows_of(ref, member):
    return ref[pl.ds(pl.multiple_of(member * OWN, OWN), OWN), :]


def prepare_kernel(
    plan_ref,
    valid_ref,
    records_ref,
    masked_ref,
    mine_ref,
    others_ref,
    pair_ref,
    low_ref,
    top_ref,
    order_ref,
):
    far = jnp.where(plan_ref[0] == FARTHEST, 0, jnp.where(plan_ref[1] == FARTHEST, 1, 2))
    first = jnp.where(far == 0, 1, 0)
    second = jnp.where(far == 2, 1, 2)
    first_bits = jnp.where(far == 0, plan_ref[1], plan_ref[0])
    second_bits = jnp.where(far == 2, plan_ref[1], plan_ref[2])
    swap = (first_bits & 7) > (second_bits & 7)
    low = jnp.where(swap, second_bits, first_bits)
    top = jnp.where(swap, first_bits, second_bits)
    a = low & 7
    pair_ref[0] = a * 8 - ((a * (a - 1)) >> 1) + (top & 7) - a
    low_ref[0] = low >> 3
    top_ref[0] = top >> 3
    order_ref[0] = far
    order_ref[1] = jnp.where(swap, second, first)
    order_ref[2] = jnp.where(swap, first, second)
    row = lax.broadcasted_iota(jnp.int32, (STA_DEV, STA_DEV), 0)
    col = lax.broadcasted_iota(jnp.int32, (STA_DEV, STA_DEV), 1)
    flags = jnp.where(row == col, valid_ref[...].astype(jnp.float32), 0.0).astype(jnp.bfloat16)
    masked = jnp.dot(flags, records_ref[...], preferred_element_type=jnp.float32)
    masked_ref[...] = masked.astype(jnp.bfloat16)
    here = lax.axis_index("tm")
    mine_ref[...] = rows_of(masked_ref, here)
    for k in range(1, TM):
        others_ref[(k - 1) * OWN : k * OWN, :] = rows_of(masked_ref, lax.rem(here + k, TM))


def prepare(plan, valid, records):
    smem = pl.BlockSpec(memory_space=pltpu.SMEM)
    vmem = pl.BlockSpec(memory_space=pltpu.VMEM)
    scalar = jax.ShapeDtypeStruct((1,), jnp.int32)
    return pl.pallas_call(
        prepare_kernel,
        out_shape=(
            jax.ShapeDtypeStruct(records.shape, jnp.bfloat16),
            jax.ShapeDtypeStruct((OWN, TILE), jnp.bfloat16),
            jax.ShapeDtypeStruct((STA_DEV - OWN, TILE), jnp.bfloat16),
            scalar,
            scalar,
            scalar,
            jax.ShapeDtypeStruct((ROUNDS,), jnp.int32),
        ),
        in_specs=[smem, vmem, vmem],
        out_specs=(vmem, vmem, vmem, smem, smem, smem, smem),
        name="prepare",
    )(plan, valid.reshape(1, STA_DEV), records)


def exchange(value, distance):
    if distance == 0:
        return value
    pairs = [(s, s ^ distance) for s in range(BLOCKS)]
    return lax.ppermute(value, "sta", pairs)


def select_branch(index, branches, *operands):
    traced = jax.make_jaxpr(lambda *args: lax.switch(args[0], branches, *args[1:]))(index, *operands)
    (cond,) = [eqn for eqn in traced.eqns if eqn.primitive.name == "cond"]
    return cond.primitive.bind(index, *operands, **cond.params)


def low_bits_pair(value, index):
    def branch(value, near, other):
        low = exchange(value, near)
        return low, low if near == other else exchange(value, other)

    branches = [
        functools.partial(branch, near=i, other=j) for i in range(8) for j in range(i, 8)
    ]
    return select_branch(index, branches, value)


def high_bits(value, index):
    branches = [functools.partial(exchange, distance=k << 3) for k in range(BLOCKS >> 3)]
    return select_branch(index, branches, value)[0]


def local(records, filter_taps, plan, station_valid):
    masked, mine, others, pair, low_index, top_index, order = prepare(plan, station_valid, records)
    far = exchange(masked, FARTHEST)
    low, top = low_bits_pair(masked, pair.reshape(()))
    top = high_bits(top, top_index.reshape(()))
    low = high_bits(low, low_index.reshape(()))
    sent = jnp.concatenate([far, low, top, others], axis=0)
    blocks = lax.all_gather(sent, "tm")
    return correlate(order, filter_taps.reshape(1, TAPS), mine, blocks)


def solution(mesh):
    return jax.shard_map(
        local,
        mesh=mesh,
        in_specs=(P("sta", "tm"), P(), P(), P("sta")),
        out_specs=P(None, ("sta", "tm"), None, None),
        check_vma=False,
    )
```

```python
import functools

import jax
import jax.numpy as jnp
from jax import lax
from jax.experimental import pallas as pl
from jax.experimental.pallas import tpu as pltpu
from jax.sharding import PartitionSpec as P

TAPS = 127
AVG_HALF = 64
LAGS = 101
HALF_LAGS = 50
SAMPLES = 1024
STA_DEV = 128
OWN = 32
ROUNDS = 3
SIDE = 128
TILE = 256
EDGE = SIDE // 2
SPAN = TILE + 2 * EDGE
WIDE = SAMPLES + SIDE
LAG_STEP = 51
LEAD_GAP = SIDE // 2 - HALF_LAGS
TM = 4
BLOCKS = 128
FARTHEST = BLOCKS - 1
SENT = ROUNDS * STA_DEV - OWN
NT = (((1,), (1,)), ((), ()))


def dot_nt(a, b):
    return lax.dot_general(a, b, NT, preferred_element_type=jnp.float32)


def split_bf16(value):
    high = value.astype(jnp.bfloat16)
    low = (value - high.astype(jnp.float32)).astype(jnp.bfloat16)
    return high, low


def bands(taps_row):
    width = 2 * TILE
    padded = jnp.concatenate([taps_row, jnp.zeros((1, width - TAPS), jnp.float32)], axis=1)
    spread = jnp.broadcast_to(padded, (TILE, width))
    rolled = pltpu.roll(spread, EDGE - (TAPS - 1) // 2, 1, stride=1, stride_axis=0)
    taps = jnp.concatenate(split_bf16(rolled[:, :SPAN]), axis=1)
    out_pos = lax.broadcasted_iota(jnp.int32, (TILE, SPAN), 0)
    in_pos = lax.broadcasted_iota(jnp.int32, (TILE, SPAN), 1)
    offset = in_pos - out_pos - EDGE
    inside = (offset >= -AVG_HALF) & (offset <= AVG_HALF)
    ones = jnp.where(inside, 1.0, 0.0).astype(jnp.bfloat16)
    return taps, jnp.concatenate([ones, ones], axis=1)


def stacked_windows(series):
    edge = jnp.zeros((series.shape[0], EDGE), series.dtype)
    extended = jnp.concatenate([edge, series, edge], axis=1)
    tiles = [extended[:, TILE * c : TILE * c + SPAN] for c in range(SAMPLES // TILE)]
    return jnp.concatenate(tiles, axis=0)


def unstacked(tiles, rows):
    return jnp.concatenate(
        [tiles[rows * c : rows * (c + 1)] for c in range(SAMPLES // TILE)], axis=1
    )


def normalize_rows(raw, taps, ones):
    rows = raw.shape[0]
    windows = stacked_windows(raw)
    filtered = unstacked(dot_nt(jnp.concatenate([windows, windows], axis=1), taps), rows)
    halves = [stacked_windows(half) for half in split_bf16(jnp.abs(filtered))]
    total = dot_nt(jnp.concatenate(halves, axis=1), ones)
    magnitude = unstacked(total, rows) / (2 * AVG_HALF + 1) + 1e-05
    return (filtered / magnitude).astype(jnp.bfloat16)


def shift_windows(own_ext, lag):
    start = SIDE - LEAD_GAP - lag
    lanes = lax.broadcasted_iota(jnp.int32, (OWN, SIDE), 1)
    near = lanes < SIDE - start
    rolled = [
        pltpu.roll(own_ext[:, SIDE * c : SIDE * (c + 1)], SIDE - start, 1)
        for c in range(WIDE // SIDE)
    ]
    return [jnp.where(near, rolled[c], rolled[c + 1]) for c in range(SAMPLES // SIDE)]


def correlate_kernel(
    order_ref, taps_ref, mine_ref, early_ref, late_ref, out_ref, own_norm, part_norm, shifted
):
    step = pl.program_id(0)

    @pl.when(step == 0)
    def _():
        taps, ones = bands(taps_ref[...])
        series = [
            jnp.concatenate(
                [early_ref[t, r * STA_DEV : (r + 1) * STA_DEV, :] for t in range(TM)], axis=1
            )
            for r in range(ROUNDS - 1)
        ]
        series.append(jnp.concatenate([late_ref[t] for t in range(TM)], axis=1))
        own = []
        for t in range(TM):
            ahead = lax.rem(lax.axis_index("tm") + TM - t, TM)
            place = (ROUNDS - 1) * STA_DEV + jnp.maximum(ahead - 1, 0) * OWN
            sent = early_ref[t, pl.ds(pl.multiple_of(place, OWN), OWN), :]
            own.append(jnp.where(ahead == 0, mine_ref[...], sent))
        series.append(jnp.concatenate(own, axis=1))
        for r in range(ROUNDS):
            part_norm[r * STA_DEV : (r + 1) * STA_DEV, :] = normalize_rows(series[r], taps, ones)
        own = normalize_rows(series[ROUNDS], taps, ones).astype(jnp.float32)
        lead = jnp.zeros((OWN, EDGE), jnp.float32)
        own_norm[...] = jnp.concatenate([lead, own, lead], axis=1).astype(jnp.bfloat16)

    for k in range(LAG_STEP):
        windows = shift_windows(own_norm, step * LAG_STEP + k)
        for c, window in enumerate(windows):
            shifted[k * OWN : (k + 1) * OWN, SIDE * c : SIDE * (c + 1)] = window.astype(jnp.bfloat16)
    sums = dot_nt(shifted[...], part_norm[...]) * (1.0 / 32.0)
    for slot in range(ROUNDS):
        block = sums[:, slot * STA_DEV : (slot + 1) * STA_DEV].astype(jnp.bfloat16)
        out_ref[order_ref[slot]] = block.reshape(LAG_STEP, OWN, STA_DEV)


def correlate(order, taps_row, mine, early, late):
    by_lag = pl.pallas_call(
        correlate_kernel,
        out_shape=jax.ShapeDtypeStruct((ROUNDS, LAGS, OWN, STA_DEV), jnp.bfloat16),
        grid_spec=pltpu.PrefetchScalarGridSpec(
            num_scalar_prefetch=1,
            grid=(pl.cdiv(LAGS, LAG_STEP),),
            in_specs=[
                pl.BlockSpec((1, TAPS), lambda i, order: (0, 0)),
                pl.BlockSpec((OWN, TILE), lambda i, order: (0, 0)),
                pl.BlockSpec((TM, SENT, TILE), lambda i, order: (0, 0, 0)),
                pl.BlockSpec((TM, STA_DEV, TILE), lambda i, order: (0, 0, 0)),
            ],
            out_specs=pl.BlockSpec(
                (ROUNDS, LAG_STEP, OWN, STA_DEV), lambda i, order: (0, i, 0, 0)
            ),
            scratch_shapes=[
                pltpu.VMEM((OWN, WIDE), jnp.bfloat16),
                pltpu.VMEM((ROUNDS * STA_DEV, SAMPLES), jnp.bfloat16),
                pltpu.VMEM((LAG_STEP * OWN, SAMPLES), jnp.bfloat16),
            ],
        ),
        compiler_params=pltpu.CompilerParams(vmem_limit_bytes=24 << 20),
        name="correlate",
    )(order, taps_row, mine, early, late)
    return jnp.transpose(by_lag, (0, 2, 1, 3))


def rows_of(ref, member):
    return ref[pl.ds(pl.multiple_of(member * OWN, OWN), OWN), :]


def prepare_kernel(
    plan_ref,
    valid_ref,
    records_ref,
    masked_ref,
    mine_ref,
    others_ref,
    pair_ref,
    low_ref,
    top_ref,
    order_ref,
):
    far = jnp.where(plan_ref[0] == FARTHEST, 0, jnp.where(plan_ref[1] == FARTHEST, 1, 2))
    first = jnp.where(far == 0, 1, 0)
    second = jnp.where(far == 2, 1, 2)
    first_bits = jnp.where(far == 0, plan_ref[1], plan_ref[0])
    second_bits = jnp.where(far == 2, plan_ref[1], plan_ref[2])
    swap = (first_bits & 7) > (second_bits & 7)
    low = jnp.where(swap, second_bits, first_bits)
    top = jnp.where(swap, first_bits, second_bits)
    a = low & 7
    pair_ref[0] = a * 8 - ((a * (a - 1)) >> 1) + (top & 7) - a
    low_ref[0] = low >> 3
    top_ref[0] = top >> 3
    order_ref[0] = far
    order_ref[1] = jnp.where(swap, second, first)
    order_ref[2] = jnp.where(swap, first, second)
    row = lax.broadcasted_iota(jnp.int32, (STA_DEV, STA_DEV), 0)
    col = lax.broadcasted_iota(jnp.int32, (STA_DEV, STA_DEV), 1)
    flags = jnp.where(row == col, valid_ref[...].astype(jnp.float32), 0.0).astype(jnp.bfloat16)
    masked = jnp.dot(flags, records_ref[...], preferred_element_type=jnp.float32)
    masked_ref[...] = masked.astype(jnp.bfloat16)
    here = lax.axis_index("tm")
    mine_ref[...] = rows_of(masked_ref, here)
    for k in range(1, TM):
        others_ref[(k - 1) * OWN : k * OWN, :] = rows_of(masked_ref, lax.rem(here + k, TM))


def prepare(plan, valid, records):
    smem = pl.BlockSpec(memory_space=pltpu.SMEM)
    vmem = pl.BlockSpec(memory_space=pltpu.VMEM)
    scalar = jax.ShapeDtypeStruct((1,), jnp.int32)
    return pl.pallas_call(
        prepare_kernel,
        out_shape=(
            jax.ShapeDtypeStruct(records.shape, jnp.bfloat16),
            jax.ShapeDtypeStruct((OWN, TILE), jnp.bfloat16),
            jax.ShapeDtypeStruct((STA_DEV - OWN, TILE), jnp.bfloat16),
            scalar,
            scalar,
            scalar,
            jax.ShapeDtypeStruct((ROUNDS,), jnp.int32),
        ),
        in_specs=[smem, vmem, vmem],
        out_specs=(vmem, vmem, vmem, smem, smem, smem, smem),
        name="prepare",
    )(plan, valid.reshape(1, STA_DEV), records)


def exchange(value, distance):
    if distance == 0:
        return value
    pairs = [(s, s ^ distance) for s in range(BLOCKS)]
    return lax.ppermute(value, "sta", pairs)


def select_branch(index, branches, *operands):
    traced = jax.make_jaxpr(lambda *args: lax.switch(args[0], branches, *args[1:]))(index, *operands)
    (cond,) = [eqn for eqn in traced.eqns if eqn.primitive.name == "cond"]
    return cond.primitive.bind(index, *operands, **cond.params)


def low_bits_pair(value, index):
    def branch(value, near, other):
        low = exchange(value, near)
        return low, low if near == other else exchange(value, other)

    branches = [
        functools.partial(branch, near=i, other=j) for i in range(8) for j in range(i, 8)
    ]
    return select_branch(index, branches, value)


def high_bits(value, index):
    branches = [functools.partial(exchange, distance=k << 3) for k in range(BLOCKS >> 3)]
    return select_branch(index, branches, value)[0]


def high_bits_and_early(value, index, early):
    def branch(value, *early, distance):
        moved = exchange(value, distance)
        return moved, lax.all_gather(jnp.concatenate(early, axis=0), "tm")

    branches = [functools.partial(branch, distance=k << 3) for k in range(BLOCKS >> 3)]
    return select_branch(index, branches, value, *early)


def local(records, filter_taps, plan, station_valid):
    masked, mine, others, pair, low_index, top_index, order = prepare(plan, station_valid, records)
    far = exchange(masked, FARTHEST)
    low, top = low_bits_pair(masked, pair.reshape(()))
    low = high_bits(low, low_index.reshape(()))
    top, early = high_bits_and_early(top, top_index.reshape(()), (far, low, others))
    late = lax.all_gather(top, "tm")
    return correlate(order, filter_taps.reshape(1, TAPS), mine, early, late)


def solution(mesh):
    return jax.shard_map(
        local,
        mesh=mesh,
        in_specs=(P("sta", "tm"), P(), P(), P("sta")),
        out_specs=P(None, ("sta", "tm"), None, None),
        check_vma=False,
    )
```
